32 devices in a mesh: ctx: 8 (over y, x, core), ch: 4 (over z).
Axes of the slice: x: 2, y: 2, z: 4, core: 2. Of those that a mesh axis runs over, the one named last changes fastest.
Arguments:
- queries: bfloat16 [8192, 2048], P('ch', 'ctx'), may hold values from -6 to 6
- keys: bfloat16 [8192, 2048], P('ch', 'ctx'), may hold values from -6 to 6
- values: bfloat16 [8192, 2048], P('ch', 'ctx'), may hold values from -6 to 6
- short_taps: float32 [3, 7, 8192], P(None, None, 'ch'), may hold values from -2 to 2
- long_filter: bfloat16 [4, 2048, 2048], P('ch', 'ctx'), may hold values from -1.5 to 1.5
- skip_gain: float32 [4, 2048], P('ch', 'ctx'), may hold values from 0.5 to 1.5
Outputs:
- mixed: bfloat16 [8192, 2048], P('ch', 'ctx')
The draws below stay inside these ranges and needn't reach their ends.
All inputs are finite; a program needn't handle non-finite values.
Results may differ from the reference program's by a relative error of at most 0.01.
Values may be sent and summed in bfloat16 or wider, within the bound.
A program may use at most 64 MiB of HBM per device.

```python
import math
import jax
import jax.numpy as jnp
from jax import lax

D = 8192
TAPS = 7
TOKENS = 2048
GROUPS = 4
GROUP_WIDTH = 2048


def draw_long_filter(key, part):
    key_noise, key_rate = jax.random.split(jax.random.fold_in(key, 11))
    noise = jnp.clip(jax.random.normal(key_noise, (GROUPS, GROUP_WIDTH, TOKENS), jnp.float32), -6.0, 6.0)
    low = math.log(0.5 / TOKENS)
    high = math.log(1.0 / 30.0)
    rates = jnp.exp(jax.random.uniform(key_rate, (GROUPS, GROUP_WIDTH, 1), jnp.float32, low, high))
    positions = jnp.arange(TOKENS, dtype=jnp.float32)
    scales = jnp.sqrt(1.0 - jnp.exp(-2.0 * rates))
    return (noise * scales * jnp.exp(-rates * positions)).astype(jnp.bfloat16)


def level_of(own_key, dims, cuts, smallest, high):
    def one(dim, parts):
        steps = jax.random.uniform(jax.random.fold_in(jax.random.fold_in(own_key, 6), dim), (parts,), jnp.float32, smallest / len(cuts), high / len(cuts))
        return jnp.repeat(jnp.exp(steps), dims[dim] // parts).reshape((-1,) + (1,) * (len(dims) - dim - 1))

    loudness = one(*cuts[0])
    for cut in cuts[1:]:
        loudness = loudness * one(*cut)
    return loudness


def gaussian(key, dims, width, most, cuts=(), kind=jnp.bfloat16):
    factor_of = level_of(key, dims, cuts, -0.22, 0.18) if cuts else 1.0
    result = jax.random.normal(key, dims, jnp.float32) * width * factor_of
    return jnp.minimum(jnp.maximum(result, -most), most).astype(kind)


def setup_inputs(seed: int = 0) -> dict:
    splits = jax.random.split(jax.random.key(seed), 7)
    return {
        "queries": gaussian(splits[0], (D, TOKENS), 1.0, 6.0, ((0, 4), (1, 8))),
        "keys": gaussian(splits[1], (D, TOKENS), 1.0, 6.0, ((0, 4), (1, 8))),
        "values": gaussian(splits[2], (D, TOKENS), 1.0, 6.0, ((0, 4), (1, 8))),
        "short_taps": gaussian(splits[3], (3, TAPS, D), TAPS ** -0.5, 2.0, ((2, 4),), jnp.float32),
        "long_filter": draw_long_filter(jax.random.fold_in(splits[6], 71), 0),
        "skip_gain": jnp.clip(0.5 + 1.0 * jax.random.uniform(splits[5], (GROUPS, GROUP_WIDTH), jnp.float32) ** level_of(splits[5], (GROUPS, GROUP_WIDTH), ((0, 4), (1, 8)), -0.2, 0.2), 0.5, 1.5),
    }


def short_conv(source, taps):
    rim = taps.shape[0] - 1
    length = source.shape[1]
    padded = jnp.pad(source.astype(jnp.float32), ((0, 0), (rim, 0)))
    total = jnp.zeros(source.shape, jnp.float32)
    for shift_j in range(taps.shape[0]):
        total = total + taps[shift_j][:, None] * padded[:, rim - shift_j:rim - shift_j + length]
    return total


def reference(queries, keys, values, short_taps, long_filter, skip_gain):
    q_short = short_conv(queries, short_taps[0]).astype(jnp.bfloat16)
    gated = (short_conv(keys, short_taps[1]) * short_conv(values, short_taps[2])).astype(jnp.bfloat16)
    filters = long_filter.reshape(D, TOKENS)
    skips = skip_gain.reshape(D)
    block = math.gcd(D, 512)
    count = D // block
    padded_len = 2 * TOKENS

    def one_block(pair):
        sig, filt = pair
        spec = jnp.fft.rfft(sig.astype(jnp.float32), n=padded_len, axis=1) * jnp.fft.rfft(filt.astype(jnp.float32), n=padded_len, axis=1)
        return jnp.fft.irfft(spec, n=padded_len, axis=1)[:, :TOKENS]

    conv = lax.map(one_block, (gated.reshape(count, block, TOKENS), filters.reshape(count, block, TOKENS)))
    long_out = (conv.reshape(D, TOKENS) + skips[:, None] * gated.astype(jnp.float32)).astype(jnp.bfloat16)
    return (q_short.astype(jnp.float32) * long_out.astype(jnp.float32)).astype(jnp.bfloat16)
```

```python
import functools
import math

import jax
import jax.numpy as jnp
import ml_dtypes
import numpy as np
from jax import lax
from jax.experimental import pallas as pl
from jax.experimental.pallas import tpu as pltpu
from jax.sharding import PartitionSpec as P

MESH = pl.DeviceIdType.MESH
LANES = 128
SLOT = 8
F32 = jnp.float32
BF16 = jnp.bfloat16


def leaf_angles(count, theta):
    if count == 1:
        return [theta]
    return leaf_angles(count // 2, theta / 2) + leaf_angles(count // 2, theta / 2 + math.pi)


def root_tables(count):
    place = np.arange(LANES, dtype=np.float64)
    tables = []
    for phi in leaf_angles(count, math.pi / 2):
        angle = place[:, None] * (phi + 2.0 * math.pi * place[None, :]) / LANES
        cos, sin = np.cos(angle), np.sin(angle)
        tables.append(np.block([[cos, sin], [-sin, cos]]))
    return np.stack(tables).astype(ml_dtypes.bfloat16)


def split_forward(coefs, theta, first, emit):
    count = len(coefs)
    if count == 1:
        emit(first, *coefs[0])
        return
    half = count // 2
    cos, sin = math.cos(theta / 2), math.sin(theta / 2)
    plus, minus = [], []
    for (lo_re, lo_im), (hi_re, hi_im) in zip(coefs[:half], coefs[half:]):
        if hi_im is None:
            re, im = cos * hi_re, sin * hi_re
            plus.append((lo_re + re, im))
            minus.append((lo_re - re, -im))
        else:
            re, im = cos * hi_re - sin * hi_im, cos * hi_im + sin * hi_re
            plus.append((lo_re + re, lo_im + im))
            minus.append((lo_re - re, lo_im - im))
    split_forward(plus, theta / 2, first, emit)
    split_forward(minus, theta / 2 + math.pi, first + half, emit)


def split_inverse(fetch, count, theta, first, real_only):
    if count == 1:
        return [fetch(first)]
    half = count // 2
    cos, sin = math.cos(theta / 2), math.sin(theta / 2)
    plus = split_inverse(fetch, half, theta / 2, first, False)
    minus = split_inverse(fetch, half, theta / 2 + math.pi, first + half, False)
    low, high = [], []
    for (p_re, p_im), (m_re, m_im) in zip(plus, minus):
        d_re, d_im = p_re - m_re, p_im - m_im
        if real_only:
            low.append((p_re + m_re, None))
            high.append((cos * d_re + sin * d_im, None))
        else:
            low.append((p_re + m_re, p_im + m_im))
            high.append((cos * d_re + sin * d_im, cos * d_im - sin * d_re))
    return low + high


def slot_matrix(shape, lane_axis, off):
    lane = lax.broadcasted_iota(jnp.int32, shape, lane_axis)
    tok = lax.broadcasted_iota(jnp.int32, shape, 1 - lane_axis)
    hit = (lane - tok == off - (LANES - SLOT)) & (tok >= LANES - SLOT)
    return hit.astype(F32).astype(BF16)


def kernel(
    n, chunks,
    q_ref, k_ref, v_ref, taps_ref, filt_ref, gain_ref, table_ref,
    out_ref,
    packed, arrived, halo, taps_t, gated, recv, spec, h_spec, back, outb, ret, qs,
    halo_sem, in_send, in_recv, in_own, out_send, out_recv, out_own,
):
    me = lax.axis_index("ctx")
    width, tok = q_ref.shape
    chan, length = filt_ref.shape
    rows = chan // chunks
    rim = taps_ref.shape[1]
    blocks = length // LANES
    tiles = tok // LANES
    sources = (q_ref, k_ref, v_ref)
    step = 16

    barrier = pltpu.get_barrier_semaphore()
    for d in range(1, n):
        pl.semaphore_signal(barrier, inc=1, device_id={"ctx": lax.rem(me + d, n)}, device_id_type=MESH)

    group = packed.shape[0]
    groups = width // group
    total = jnp.zeros(packed.shape, F32)
    for g in range(groups):
        for w in range(3):
            pick = slot_matrix((LANES, packed.shape[1]), 1, g * 32 + w * SLOT)
            tail = sources[w][g * group : (g + 1) * group, tok - LANES :]
            total = total + jnp.dot(tail, pick, preferred_element_type=F32)
    packed[...] = total.astype(BF16)

    pl.semaphore_wait(barrier, n - 1)

    def taps_step(g, _):
        at = pl.ds(pl.multiple_of(g * LANES, LANES), LANES)
        stack = [taps_ref[w, :, at] for w in range(3)]
        blank = jnp.zeros((SLOT - rim, LANES), F32)
        parts = []
        for one in stack:
            parts += [one, blank]
        parts.append(jnp.zeros((LANES - 3 * SLOT, LANES), F32))
        taps_t[at, :] = jnp.transpose(jnp.concatenate(parts, axis=0))
        return 0

    halo_copy = pltpu.make_async_remote_copy(
        src_ref=packed, dst_ref=arrived, send_sem=halo_sem.at[0], recv_sem=halo_sem.at[1],
        device_id={"ctx": lax.rem(me + 1, n)}, device_id_type=MESH,
    )
    lax.fori_loop(0, width // LANES, taps_step, 0)
    halo_copy.start()

    def emit_at(at):
        def emit(leaf, re, im):
            spec[leaf, at, :LANES] = re.astype(BF16)
            spec[leaf, at, LANES:] = im.astype(BF16)

        return emit

    def filt_step(r, _):
        at = pl.ds(pl.multiple_of(r * step, step), step)
        coefs = [(filt_ref[at, a * LANES : (a + 1) * LANES].astype(F32), None) for a in range(blocks)]
        split_forward(coefs, math.pi / 2, 0, emit_at(at))
        return 0

    lax.fori_loop(0, chan // step, filt_step, 0)

    def filt_leaf(leaf, _):
        h_spec[leaf] = jnp.dot(spec[leaf], table_ref[leaf], preferred_element_type=F32)
        return 0

    lax.fori_loop(0, blocks, filt_leaf, 0)

    halo_copy.wait()
    for g in range(groups):
        for w in range(3):
            spread = slot_matrix((packed.shape[1], LANES), 0, g * 32 + w * SLOT)
            got = jnp.dot(arrived[...], spread, preferred_element_type=F32)
            halo[w, g * group : (g + 1) * group, :] = jnp.where(me > 0, got, 0.0).astype(BF16)

    def short(w, at):
        src = sources[w]
        lane = lax.broadcasted_iota(jnp.int32, (step, LANES), 1)
        parts = [halo[w, at, :].astype(F32)]
        parts += [src[at, t * LANES : (t + 1) * LANES].astype(F32) for t in range(tiles)]
        sums = [None] * tiles
        for j in range(rim):
            tap = jnp.broadcast_to(taps_t[at, w * SLOT + j : w * SLOT + j + 1], (step, LANES))
            turned = parts if j == 0 else [pltpu.roll(p, j, 1) for p in parts]
            for t in range(tiles):
                x = turned[t + 1] if j == 0 else jnp.where(lane < j, turned[t], turned[t + 1])
                sums[t] = tap * x if j == 0 else sums[t] + tap * x
        return sums

    def cols(t):
        return slice(t * LANES, (t + 1) * LANES)

    def gate_rows(base, count):
        def one(r, _):
            at = pl.ds(pl.multiple_of(base + r * step, step), step)
            keys, values = short(1, at), short(2, at)
            for t in range(tiles):
                gated[at, cols(t)] = (keys[t] * values[t]).astype(BF16)
            return 0

        lax.fori_loop(0, count // step, one, 0)

    def peer_rows(peer, c):
        return pl.ds(pl.multiple_of(peer * chan + c * rows, rows), rows)

    def chunk_rows(c):
        return pl.ds(pl.multiple_of(c * rows, rows), rows)

    def in_copy(c, d):
        peer = lax.rem(me + d, n)
        return pltpu.make_async_remote_copy(
            src_ref=gated.at[peer_rows(peer, c), :], dst_ref=recv.at[me, chunk_rows(c), :],
            send_sem=in_send.at[c, d], recv_sem=in_recv.at[c, d],
            device_id={"ctx": peer}, device_id_type=MESH,
        )

    def own_in(c):
        return pltpu.make_async_copy(gated.at[peer_rows(me, c), :], recv.at[me, chunk_rows(c), :], in_own.at[c])

    def out_copy(c, d):
        peer = lax.rem(me + d, n)
        return pltpu.make_async_remote_copy(
            src_ref=outb.at[peer, chunk_rows(c), :], dst_ref=ret.at[peer_rows(me, c), :],
            send_sem=out_send.at[c, d], recv_sem=out_recv.at[c, d],
            device_id={"ctx": peer}, device_id_type=MESH,
        )

    def own_out(c):
        return pltpu.make_async_copy(outb.at[me, chunk_rows(c), :], ret.at[peer_rows(me, c), :], out_own.at[c])

    for c in range(chunks):
        def send_step(d, _):
            gate_rows(lax.rem(me + d, n) * chan + c * rows, rows)

            @pl.when(d > 1)
            def _():
                in_copy(c, d - 1).start()

            return 0

        lax.fori_loop(1, n, send_step, 0)
        gate_rows(me * chan + c * rows, rows)
        in_copy(c, n - 1).start()
        own_in(c).start()

    def q_step(r, _):
        at = pl.ds(pl.multiple_of(r * step, step), step)
        sums = short(0, at)
        for t in range(tiles):
            qs[at, cols(t)] = sums[t].astype(BF16)
        return 0

    lax.fori_loop(0, width // step, q_step, 0)

    for c in range(chunks):
        def wait_in(d, _):
            in_copy(c, d).wait()
            return 0

        lax.fori_loop(1, n, wait_in, 0)
        own_in(c).wait()

        def sig_step(r, _):
            at = pl.ds(pl.multiple_of(c * rows + r * step, step), step)
            coefs = [(recv[a // tiles, at, cols(a % tiles)].astype(F32), None) for a in range(blocks)]
            split_forward(coefs, math.pi / 2, 0, emit_at(at))
            return 0

        lax.fori_loop(0, rows // step, sig_step, 0)

        def leaf_step(leaf, _):
            at = slice(c * rows, (c + 1) * rows)
            table = table_ref[leaf]
            sig = jnp.dot(spec[leaf, at, :], table, preferred_element_type=F32)
            h_re, h_im = h_spec[leaf, at, :LANES], h_spec[leaf, at, LANES:]
            s_re, s_im = sig[:, :LANES], sig[:, LANES:]
            prod = jnp.concatenate([s_re * h_re - s_im * h_im, s_re * h_im + s_im * h_re], axis=1).astype(BF16)
            back[leaf] = lax.dot_general(prod, table, (((1,), (1,)), ((), ())), preferred_element_type=F32)
            return 0

        lax.fori_loop(0, blocks, leaf_step, 0)

        def back_step(r, _):
            at = pl.ds(pl.multiple_of(r * step, step), step)
            whole = pl.ds(pl.multiple_of(c * rows + r * step, step), step)
            row = lax.broadcasted_iota(jnp.int32, (step, chan), 0) + (c * rows + r * step)
            col = lax.broadcasted_iota(jnp.int32, (step, chan), 1)
            gain = jnp.sum(jnp.where(row == col, gain_ref[...], 0.0), axis=1, keepdims=True)
            gain = jnp.broadcast_to(gain, (step, LANES))
            parts = split_inverse(
                lambda leaf: (back[leaf, at, :LANES], back[leaf, at, LANES:]), blocks, math.pi / 2, 0, True
            )
            for a, (re, _unused) in enumerate(parts):
                sig = recv[a // tiles, whole, cols(a % tiles)].astype(F32)
                outb[a // tiles, whole, cols(a % tiles)] = (re * (1.0 / length) + gain * sig).astype(BF16)
            return 0

        lax.fori_loop(0, rows // step, back_step, 0)

        def return_step(d, _):
            out_copy(c, d).start()
            return 0

        lax.fori_loop(1, n, return_step, 0)
        own_out(c).start()

    def mix_rows(base):
        at = pl.ds(pl.multiple_of(base, rows), rows)
        out_ref[at, :] = (qs[at, :].astype(F32) * ret[at, :].astype(F32)).astype(BF16)

    for c in range(chunks):
        own_out(c).wait()
        mix_rows(me * chan + c * rows)

        def mix_step(d, _):
            out_copy(c, d).wait()
            mix_rows(lax.rem(me + n - d, n) * chan + c * rows)
            return 0

        lax.fori_loop(1, n, mix_step, 0)


def solution(mesh):
    n = mesh.shape["ctx"]

    def local(queries, keys, values, short_taps, long_filter, skip_gain):
        width, tok = queries.shape
        chan, length = long_filter.shape[1:]
        blocks = length // LANES
        chunks = 2
        table = jnp.asarray(root_tables(blocks))
        dma = pltpu.SemaphoreType.DMA
        two = 2 * LANES
        groups = 8
        return pl.pallas_call(
            functools.partial(kernel, n, chunks),
            out_shape=jax.ShapeDtypeStruct((width, tok), BF16),
            in_specs=[pl.BlockSpec(memory_space=pltpu.VMEM)] * 7,
            out_specs=pl.BlockSpec(memory_space=pltpu.VMEM),
            scratch_shapes=[
                pltpu.VMEM((width // groups, 32 * groups), BF16),
                pltpu.VMEM((width // groups, 32 * groups), BF16),
                pltpu.VMEM((3, width, LANES), BF16),
                pltpu.VMEM((width, LANES), F32),
                pltpu.VMEM((width, tok), BF16),
                pltpu.VMEM((n, chan, tok), BF16),
                pltpu.VMEM((blocks, chan, two), BF16),
                pltpu.VMEM((blocks, chan, two), F32),
                pltpu.VMEM((blocks, chan // chunks, two), F32),
                pltpu.VMEM((n, chan, tok), BF16),
                pltpu.VMEM((width, tok), BF16),
                pltpu.VMEM((width, tok), BF16),
                dma((2,)),
                dma((chunks, n)),
                dma((chunks, n)),
                dma((chunks,)),
                dma((chunks, n)),
                dma((chunks, n)),
                dma((chunks,)),
            ],
            compiler_params=pltpu.CompilerParams(
                collective_id=0, has_side_effects=True, vmem_limit_bytes=60 * 1024 * 1024
            ),
            name="hyena",
        )(queries, keys, values, short_taps, long_filter[0], skip_gain, table)

    placed = (
        P("ch", "ctx"),
        P("ch", "ctx"),
        P("ch", "ctx"),
        P(None, None, "ch"),
        P("ch", "ctx", None),
        P("ch", "ctx"),
    )
    return jax.shard_map(local, mesh=mesh, in_specs=placed, out_specs=P("ch", "ctx"), check_vma=False)
```

```python
import functools
import math

import jax
import jax.numpy as jnp
import ml_dtypes
import numpy as np
from jax import lax
from jax.experimental import pallas as pl
from jax.experimental.pallas import tpu as pltpu
from jax.sharding import PartitionSpec as P

MESH = pl.DeviceIdType.MESH
LANES = 128
SLOT = 8
F32 = jnp.float32
BF16 = jnp.bfloat16


def leaf_angles(count, theta):
    if count == 1:
        return [theta]
    return leaf_angles(count // 2, theta / 2) + leaf_angles(count // 2, theta / 2 + math.pi)


def root_tables(count):
    place = np.arange(LANES, dtype=np.float64)
    tables = []
    for phi in leaf_angles(count, math.pi / 2):
        angle = place[:, None] * (phi + 2.0 * math.pi * place[None, :]) / LANES
        cos, sin = np.cos(angle), np.sin(angle)
        tables.append(np.block([[cos, sin], [-sin, cos]]).T)
    return np.stack(tables).astype(ml_dtypes.bfloat16)


def split_forward(coefs, theta, first, emit):
    count = len(coefs)
    if count == 1:
        emit(first, *coefs[0])
        return
    half = count // 2
    cos, sin = math.cos(theta / 2), math.sin(theta / 2)
    plus, minus = [], []
    for (lo_re, lo_im), (hi_re, hi_im) in zip(coefs[:half], coefs[half:]):
        if hi_im is None:
            re, im = cos * hi_re, sin * hi_re
            plus.append((lo_re + re, im))
            minus.append((lo_re - re, -im))
        else:
            re, im = cos * hi_re - sin * hi_im, cos * hi_im + sin * hi_re
            plus.append((lo_re + re, lo_im + im))
            minus.append((lo_re - re, lo_im - im))
    split_forward(plus, theta / 2, first, emit)
    split_forward(minus, theta / 2 + math.pi, first + half, emit)


def split_inverse(fetch, count, theta, first, real_only):
    if count == 1:
        return [fetch(first)]
    half = count // 2
    cos, sin = math.cos(theta / 2), math.sin(theta / 2)
    plus = split_inverse(fetch, half, theta / 2, first, False)
    minus = split_inverse(fetch, half, theta / 2 + math.pi, first + half, False)
    low, high = [], []
    for (p_re, p_im), (m_re, m_im) in zip(plus, minus):
        d_re, d_im = p_re - m_re, p_im - m_im
        if real_only:
            low.append((p_re + m_re, None))
            high.append((cos * d_re + sin * d_im, None))
        else:
            low.append((p_re + m_re, p_im + m_im))
            high.append((cos * d_re + sin * d_im, cos * d_im - sin * d_re))
    return low + high


def across(eye, block):
    return lax.dot_general(eye, block, (((1,), (1,)), ((), ())), preferred_element_type=F32)


def kernel(
    n, lanes,
    q_ref, k_ref, v_ref, taps_ref, filt_ref, gain_ref, table_ref,
    out_ref,
    eye, tails, halo, turned, gated, recv, spec, h_spec, ret, back_table,
    halo_sem, in_send, in_recv, in_own, out_send, out_recv, out_own,
):
    me = lax.axis_index("ctx")
    width, tok = q_ref.shape
    chan, length = filt_ref.shape
    chunks = chan // lanes
    rim = taps_ref.shape[-2]
    blocks = length // LANES
    tiles = tok // LANES
    sources = (q_ref, k_ref, v_ref)
    step = 16

    barrier = pltpu.get_barrier_semaphore()
    for d in range(1, n):
        pl.semaphore_signal(barrier, inc=1, device_id={"ctx": lax.rem(me + d, n)}, device_id_type=MESH)

    side = eye.shape[0]
    row = lax.broadcasted_iota(jnp.int32, (side, side), 0)
    col = lax.broadcasted_iota(jnp.int32, (side, side), 1)
    eye[...] = (row == col).astype(F32).astype(BF16)

    pick_row = lax.broadcasted_iota(jnp.int32, (SLOT, LANES), 0) + (LANES - SLOT)
    pick = (pick_row == lax.broadcasted_iota(jnp.int32, (SLOT, LANES), 1)).astype(F32).astype(BF16)

    def tail_step(p, _):
        at = pl.ds(pl.multiple_of(p * chan, chan), chan)
        for w in range(3):
            tails[w, p] = across(pick, sources[w][at, tok - LANES :]).astype(BF16)
        return 0

    lax.fori_loop(0, n, tail_step, 0)

    pl.semaphore_wait(barrier, n - 1)
    halo_copy = pltpu.make_async_remote_copy(
        src_ref=tails, dst_ref=halo, send_sem=halo_sem.at[0], recv_sem=halo_sem.at[1],
        device_id={"ctx": lax.rem(me + 1, n)}, device_id_type=MESH,
    )

    for a in range(blocks):
        gated[a // tiles, (a % tiles) * LANES : (a % tiles + 1) * LANES, :] = across(
            eye[:LANES, :LANES], filt_ref[:, a * LANES : (a + 1) * LANES]
        ).astype(BF16)
    halo_copy.start()

    def short_stage(ref, at_lanes):
        def one(r, _):
            def emit(leaf, re, im):
                spec[leaf, pl.ds(pl.multiple_of(r * step, step), step), at_lanes] = re.astype(BF16)
                spec[leaf, pl.ds(pl.multiple_of(LANES + r * step, step), step), at_lanes] = im.astype(BF16)

            coefs = []
            for a in range(blocks):
                at = pl.ds(pl.multiple_of((a % tiles) * LANES + r * step, step), step)
                coefs.append((ref[a // tiles, at, at_lanes].astype(F32), None))
            split_forward(coefs, math.pi / 2, 0, emit)
            return 0

        lax.fori_loop(0, LANES // step, one, 0)

    def chunk_lanes(c):
        return slice(c * lanes, (c + 1) * lanes)

    for c in range(chunks):
        short_stage(gated, chunk_lanes(c))

    def filt_leaf(leaf, _):
        table = table_ref[leaf]
        h_spec[leaf] = jnp.dot(table, spec[leaf], preferred_element_type=F32).astype(h_spec.dtype)
        if back_table.shape[0] == blocks:
            back_table[leaf] = across(eye[: 2 * LANES, : 2 * LANES], table).astype(BF16)
        return 0

    lax.fori_loop(0, blocks, filt_leaf, 0, unroll=2)

    halo_copy.wait()

    def peer_rows(peer, c):
        return pl.ds(pl.multiple_of(peer * chan + c * lanes, lanes), lanes)

    def short(w, peer, c):
        turned[w, :SLOT, :] = jnp.where(me > 0, halo[w, peer, :, chunk_lanes(c)].astype(F32), 0.0)
        turned[w, SLOT:, :] = across(eye[:tok, :tok], sources[w][peer_rows(peer, c), :])
        if len(taps_ref.shape) == 3:
            taps = taps_ref[w, :, peer_rows(peer, c)]
        else:
            taps = taps_ref[peer, w, :, chunk_lanes(c)]
        return taps

    def sums_of(w, taps, start, count):
        total = None
        for j in range(rim):
            term = taps[j : j + 1, :] * turned[w, SLOT - j + start : SLOT - j + start + count, :]
            total = term if total is None else total + term
        return total

    part = 64

    def gate(peer, c):
        k_taps, v_taps = short(1, peer, c), short(2, peer, c)
        for start in range(0, tok, part):
            product = sums_of(1, k_taps, start, part) * sums_of(2, v_taps, start, part)
            gated[peer, start : start + part, chunk_lanes(c)] = product.astype(BF16)

    def in_copy(c, d):
        peer = lax.rem(me + d, n)
        return pltpu.make_async_remote_copy(
            src_ref=gated.at[peer, :, chunk_lanes(c)], dst_ref=recv.at[me, :, chunk_lanes(c)],
            send_sem=in_send.at[c, d], recv_sem=in_recv.at[c, d],
            device_id={"ctx": peer}, device_id_type=MESH,
        )

    def own_in(c):
        return pltpu.make_async_copy(gated.at[me, :, chunk_lanes(c)], recv.at[me, :, chunk_lanes(c)], in_own.at[c])

    def out_copy(c, d):
        peer = lax.rem(me + d, n)
        return pltpu.make_async_remote_copy(
            src_ref=recv.at[peer, :, chunk_lanes(c)], dst_ref=ret.at[me, :, chunk_lanes(c)],
            send_sem=out_send.at[c, d], recv_sem=out_recv.at[c, d],
            device_id={"ctx": peer}, device_id_type=MESH,
        )

    def own_out(c):
        return pltpu.make_async_copy(recv.at[me, :, chunk_lanes(c)], ret.at[me, :, chunk_lanes(c)], out_own.at[c])

    for c in range(chunks):
        def send_step(d, _):
            gate(lax.rem(me + d, n), c)

            @pl.when(d > 1)
            def _():
                in_copy(c, d - 1).start()

            return 0

        lax.fori_loop(1, n, send_step, 0)
        gate(me, c)
        in_copy(c, n - 1).start()
        own_in(c).start()

    for c in range(chunks):
        def q_step(p, _):
            taps = short(0, p, c)
            parts = [sums_of(0, taps, start, part).astype(BF16) for start in range(0, tok, part)]
            out_ref[peer_rows(p, c), :] = across(eye[:lanes, :lanes], jnp.concatenate(parts, axis=0)).astype(BF16)
            return 0

        lax.fori_loop(0, n, q_step, 0)

    for c in range(chunks):
        def wait_in(d, _):
            in_copy(c, d).wait()
            return 0

        lax.fori_loop(1, n, wait_in, 0)
        own_in(c).wait()
        at_lanes = chunk_lanes(c)
        short_stage(recv, at_lanes)

        def leaf_step(leaf, _):
            table = table_ref[leaf]
            if back_table.shape[0] == blocks:
                turn = back_table[leaf]
            else:
                turn = across(eye[: 2 * LANES, : 2 * LANES], table).astype(BF16)
            sig = jnp.dot(table, spec[leaf, :, at_lanes], preferred_element_type=F32)
            h_re, h_im = h_spec[leaf, :LANES, at_lanes].astype(F32), h_spec[leaf, LANES:, at_lanes].astype(F32)
            s_re, s_im = sig[:LANES], sig[LANES:]
            prod = jnp.concatenate([s_re * h_re - s_im * h_im, s_re * h_im + s_im * h_re], axis=0).astype(BF16)
            h_spec[leaf, :, at_lanes] = jnp.dot(turn, prod, preferred_element_type=F32).astype(h_spec.dtype)
            return 0

        lax.fori_loop(0, blocks, leaf_step, 0, unroll=4)
        gain = gain_ref[:, at_lanes]

        def back_step(r, _):
            re_at = pl.ds(pl.multiple_of(r * step, step), step)
            im_at = pl.ds(pl.multiple_of(LANES + r * step, step), step)
            parts = split_inverse(
                lambda leaf: (h_spec[leaf, re_at, at_lanes].astype(F32), h_spec[leaf, im_at, at_lanes].astype(F32)),
                blocks, math.pi / 2, 0, True,
            )
            for a, (re, _unused) in enumerate(parts):
                at = pl.ds(pl.multiple_of((a % tiles) * LANES + r * step, step), step)
                sig = recv[a // tiles, at, at_lanes].astype(F32)
                recv[a // tiles, at, at_lanes] = (re * (1.0 / length) + gain * sig).astype(BF16)
            return 0

        lax.fori_loop(0, LANES // step, back_step, 0)

        def return_step(d, _):
            out_copy(c, d).start()
            return 0

        lax.fori_loop(1, n, return_step, 0)
        own_out(c).start()

    def mix(peer, c):
        at = peer_rows(peer, c)
        long = across(eye[:lanes, :lanes], ret[peer, :, chunk_lanes(c)])
        out_ref[at, :] = (out_ref[at, :].astype(F32) * long).astype(BF16)

    for c in range(chunks):
        own_out(c).wait()
        mix(me, c)

        def mix_step(d, _):
            out_copy(c, d).wait()
            mix(lax.rem(me + n - d, n), c)
            return 0

        lax.fori_loop(1, n, mix_step, 0)


def solution(mesh):
    n = mesh.shape["ctx"]

    def local(queries, keys, values, short_taps, long_filter, skip_gain):
        width, tok = queries.shape
        chan, length = long_filter.shape[1:]
        blocks = length // LANES
        lanes = min(chan, LANES)
        chunks = chan // lanes
        table = jnp.asarray(root_tables(blocks))
        dma = pltpu.SemaphoreType.DMA
        two = 2 * LANES
        small = blocks * two * max(chan, LANES) * 4 <= 8 * 2**20
        side = max(tok, two)
        taps = short_taps
        if lanes < LANES:
            taps = jnp.moveaxis(short_taps.reshape(3, -1, n, chan), 2, 0)
        return pl.pallas_call(
            functools.partial(kernel, n, lanes),
            out_shape=jax.ShapeDtypeStruct((width, tok), BF16),
            in_specs=[pl.BlockSpec(memory_space=pltpu.VMEM)] * 7,
            out_specs=pl.BlockSpec(memory_space=pltpu.VMEM),
            scratch_shapes=[
                pltpu.VMEM((side, side), BF16),
                pltpu.VMEM((3, n, SLOT, chan), BF16),
                pltpu.VMEM((3, n, SLOT, chan), BF16),
                pltpu.VMEM((3, SLOT + tok, lanes), F32),
                pltpu.VMEM((n, tok, chan), BF16),
                pltpu.VMEM((n, tok, chan), BF16),
                pltpu.VMEM((blocks, two, chan), BF16),
                pltpu.VMEM((blocks, two, chan), F32 if small else BF16),
                pltpu.VMEM((n, tok, chan), BF16),
                pltpu.VMEM((blocks if small else 1, two, two), BF16),
                dma((2,)),
                dma((chunks, n)),
                dma((chunks, n)),
                dma((chunks,)),
                dma((chunks, n)),
                dma((chunks, n)),
                dma((chunks,)),
            ],
            compiler_params=pltpu.CompilerParams(
                collective_id=0, has_side_effects=True, vmem_limit_bytes=67043328
            ),
            name="hyena",
        )(queries, keys, values, taps, long_filter[0], skip_gain, table)

    placed = (
        P("ch", "ctx"),
        P("ch", "ctx"),
        P("ch", "ctx"),
        P(None, None, "ch"),
        P("ch", "ctx", None),
        P("ch", "ctx"),
    )
    return jax.shard_map(local, mesh=mesh, in_specs=placed, out_specs=P("ch", "ctx"), check_vma=False)
```

```python
import functools
import math

import jax
import jax.numpy as jnp
import ml_dtypes
import numpy as np
from jax import lax
from jax.experimental import pallas as pl
from jax.experimental.pallas import tpu as pltpu
from jax.sharding import PartitionSpec as P

MESH = pl.DeviceIdType.MESH
LANES = 128
SLOT = 8
F32 = jnp.float32
BF16 = jnp.bfloat16


def leaf_angles(count, theta):
    if count == 1:
        return [theta]
    return leaf_angles(count // 2, theta / 2) + leaf_angles(count // 2, theta / 2 + math.pi)


def circle_tables():
    place = np.arange(LANES, dtype=np.float64)
    angle = place[:, None] * place[None, :] * (2.0 * math.pi / LANES)
    cos, sin = np.cos(angle), np.sin(angle)
    there = np.block([[cos, -sin], [sin, cos]])
    return np.stack([there, there.T]).astype(ml_dtypes.bfloat16)


def twist_columns(count):
    angle = np.arange(LANES)[:, None] * np.array(leaf_angles(count, math.pi / 2))[None, :] / LANES
    return np.concatenate([np.cos(angle), np.sin(angle)], axis=1).astype(np.float32)


def split_forward(coefs, theta, first, emit):
    count = len(coefs)
    if count == 1:
        emit(first, *coefs[0])
        return
    half = count // 2
    cos, sin = math.cos(theta / 2), math.sin(theta / 2)
    plus, minus = [], []
    for (lo_re, lo_im), (hi_re, hi_im) in zip(coefs[:half], coefs[half:]):
        if hi_im is None:
            re, im = cos * hi_re, sin * hi_re
            plus.append((lo_re + re, im))
            minus.append((lo_re - re, -im))
        else:
            re, im = cos * hi_re - sin * hi_im, cos * hi_im + sin * hi_re
            plus.append((lo_re + re, lo_im + im))
            minus.append((lo_re - re, lo_im - im))
    split_forward(plus, theta / 2, first, emit)
    split_forward(minus, theta / 2 + math.pi, first + half, emit)


def split_inverse(fetch, count, theta, first, real_only):
    if count == 1:
        return [fetch(first)]
    half = count // 2
    cos, sin = math.cos(theta / 2), math.sin(theta / 2)
    plus = split_inverse(fetch, half, theta / 2, first, False)
    minus = split_inverse(fetch, half, theta / 2 + math.pi, first + half, False)
    low, high = [], []
    for (p_re, p_im), (m_re, m_im) in zip(plus, minus):
        d_re, d_im = p_re - m_re, p_im - m_im
        if real_only:
            low.append((p_re + m_re, None))
            high.append((cos * d_re + sin * d_im, None))
        else:
            low.append((p_re + m_re, p_im + m_im))
            high.append((cos * d_re + sin * d_im, cos * d_im - sin * d_re))
    return low + high


def across(eye, block):
    return lax.dot_general(eye, block, (((1,), (1,)), ((), ())), preferred_element_type=F32)


def kernel(
    n, lanes,
    q_ref, k_ref, v_ref, taps_ref, filt_hbm, gain_ref, table_ref, twist_ref,
    out_ref,
    eye, tails, halo, turned, gated, recv, spec, h_spec, ret, filt_ref, filt_rows, twist,
    filt_sem, halo_sem, in_send, in_recv, in_own, out_send, out_recv, out_own,
):
    me = lax.axis_index("ctx")
    width, tok = q_ref.shape
    chan, length = filt_ref.shape
    chunks = chan // lanes
    rim = taps_ref.shape[-2]
    blocks = length // LANES
    tiles = tok // LANES
    sources = (q_ref, k_ref, v_ref)
    step = 16
    filt_copy = pltpu.make_async_copy(filt_hbm, filt_ref, filt_sem)
    filt_copy.start()

    barrier = pltpu.get_barrier_semaphore()
    for d in range(1, n):
        pl.semaphore_signal(barrier, inc=1, device_id={"ctx": lax.rem(me + d, n)}, device_id_type=MESH)

    side = eye.shape[0]
    row = lax.broadcasted_iota(jnp.int32, (side, side), 0)
    col = lax.broadcasted_iota(jnp.int32, (side, side), 1)
    eye[...] = (row == col).astype(F32).astype(BF16)

    pick_row = lax.broadcasted_iota(jnp.int32, (SLOT, LANES), 0) + (LANES - SLOT)
    pick = (pick_row == lax.broadcasted_iota(jnp.int32, (SLOT, LANES), 1)).astype(F32).astype(BF16)

    def tail_step(p, _):
        at = pl.ds(pl.multiple_of(p * chan, chan), chan)
        for w in range(3):
            tails[w, p] = across(pick, sources[w][at, tok - LANES :]).astype(BF16)
        return 0

    lax.fori_loop(0, n, tail_step, 0)

    pl.semaphore_wait(barrier, n - 1)
    halo_copy = pltpu.make_async_remote_copy(
        src_ref=tails, dst_ref=halo, send_sem=halo_sem.at[0], recv_sem=halo_sem.at[1],
        device_id={"ctx": lax.rem(me + 1, n)}, device_id_type=MESH,
    )

    for leaf in range(blocks):
        for part in range(2):
            column = twist_ref[:, part * blocks + leaf : part * blocks + leaf + 1]
            twist[leaf, part] = jnp.broadcast_to(column, (LANES, lanes))
    halo_copy.start()
    if lanes < LANES:
        spec[...] = jnp.zeros_like(spec)

    filt_copy.wait()
    for a in range(blocks):
        filt_rows[a // tiles, (a % tiles) * LANES : (a % tiles + 1) * LANES, :] = across(
            eye[:LANES, :LANES], filt_ref[:, a * LANES : (a + 1) * LANES]
        ).astype(BF16)

    def chunk_lanes(c):
        return slice(c * lanes, (c + 1) * lanes)

    def leaf_lanes(leaf):
        return slice((leaf % 2) * LANES, (leaf % 2) * LANES + lanes)

    def short_stage(ref, c):
        at_lanes = chunk_lanes(c)

        def one(r, _):
            re_at = pl.ds(pl.multiple_of(r * step, step), step)
            im_at = pl.ds(pl.multiple_of(LANES + r * step, step), step)

            def emit(leaf, re, im):
                cos, sin = twist[leaf, 0, re_at, :], twist[leaf, 1, re_at, :]
                spec[leaf // 2, re_at, leaf_lanes(leaf)] = (re * cos - im * sin).astype(BF16)
                spec[leaf // 2, im_at, leaf_lanes(leaf)] = (re * sin + im * cos).astype(BF16)

            coefs = []
            for a in range(blocks):
                at = pl.ds(pl.multiple_of((a % tiles) * LANES + r * step, step), step)
                coefs.append((ref[a // tiles, at, at_lanes].astype(F32), None))
            split_forward(coefs, math.pi / 2, 0, emit)
            return 0

        lax.fori_loop(0, LANES // step, one, 0)

    def filter_chunk(c):
        short_stage(filt_rows, c)

        def filt_pair(pair, _):
            h_spec[c, pair] = jnp.dot(table_ref[0], spec[pair], preferred_element_type=F32).astype(h_spec.dtype)
            return 0

        lax.fori_loop(0, blocks // 2, filt_pair, 0, unroll=2)

    filter_chunk(0)
    halo_copy.wait()

    def peer_rows(peer, c):
        return pl.ds(pl.multiple_of(peer * chan + c * lanes, lanes), lanes)

    def short(w, slot, peer, c):
        turned[slot, :SLOT, :] = jnp.where(me > 0, halo[w, peer, :, chunk_lanes(c)].astype(F32), 0.0)
        turned[slot, SLOT:, :] = across(eye[:tok, :tok], sources[w][peer_rows(peer, c), :])
        if len(taps_ref.shape) == 3:
            return taps_ref[w, :, peer_rows(peer, c)]
        return taps_ref[peer, w, :, chunk_lanes(c)]

    def sums_of(slot, taps, start, count):
        total = None
        for j in range(rim):
            term = taps[j : j + 1, :] * turned[slot, SLOT - j + start : SLOT - j + start + count, :]
            total = term if total is None else total + term
        return total

    part = 64

    def gate_pair(peers, c):
        taps = [(short(1, 2 * i, p, c), short(2, 2 * i + 1, p, c)) for i, p in enumerate(peers)]
        for i, p in enumerate(peers):
            for start in range(0, tok, part):
                product = sums_of(2 * i, taps[i][0], start, part) * sums_of(2 * i + 1, taps[i][1], start, part)
                gated[p, start : start + part, chunk_lanes(c)] = product.astype(BF16)

    def in_copy(c, d):
        peer = lax.rem(me + d, n)
        return pltpu.make_async_remote_copy(
            src_ref=gated.at[peer, :, chunk_lanes(c)], dst_ref=recv.at[me, :, chunk_lanes(c)],
            send_sem=in_send.at[c, d], recv_sem=in_recv.at[c, d],
            device_id={"ctx": peer}, device_id_type=MESH,
        )

    def own_in(c):
        return pltpu.make_async_copy(gated.at[me, :, chunk_lanes(c)], recv.at[me, :, chunk_lanes(c)], in_own.at[c])

    def out_copy(c, d):
        peer = lax.rem(me + d, n)
        return pltpu.make_async_remote_copy(
            src_ref=recv.at[peer, :, chunk_lanes(c)], dst_ref=ret.at[me, :, chunk_lanes(c)],
            send_sem=out_send.at[c, d], recv_sem=out_recv.at[c, d],
            device_id={"ctx": peer}, device_id_type=MESH,
        )

    def own_out(c):
        return pltpu.make_async_copy(recv.at[me, :, chunk_lanes(c)], ret.at[me, :, chunk_lanes(c)], out_own.at[c])

    for c in range(chunks):
        def send_step(i, _):
            gate_pair([lax.rem(me + 2 * i + 1, n), lax.rem(me + 2 * i + 2, n)], c)

            @pl.when(i > 0)
            def _():
                in_copy(c, 2 * i - 1).start()
                in_copy(c, 2 * i).start()

            return 0

        lax.fori_loop(0, n // 2, send_step, 0)
        in_copy(c, n - 1).start()
        own_in(c).start()

    for c in range(1, chunks):
        filter_chunk(c)

    for c in range(chunks):
        def wait_in(d, _):
            in_copy(c, d).wait()
            return 0

        lax.fori_loop(1, n, wait_in, 0)
        own_in(c).wait()
        at_lanes = chunk_lanes(c)
        short_stage(recv, c)

        def pair_step(pair, _):
            sig = jnp.dot(table_ref[0], spec[pair], preferred_element_type=F32)
            h_re, h_im = h_spec[c, pair, :LANES, :].astype(F32), h_spec[c, pair, LANES:, :].astype(F32)
            s_re, s_im = sig[:LANES], sig[LANES:]
            prod = jnp.concatenate([s_re * h_re - s_im * h_im, s_re * h_im + s_im * h_re], axis=0).astype(BF16)
            h_spec[c, pair] = jnp.dot(table_ref[1], prod, preferred_element_type=F32).astype(h_spec.dtype)
            return 0

        lax.fori_loop(0, blocks // 2, pair_step, 0, unroll=4)
        gain = gain_ref[:, at_lanes]

        def back_step(r, _):
            re_at = pl.ds(pl.multiple_of(r * step, step), step)
            im_at = pl.ds(pl.multiple_of(LANES + r * step, step), step)
            def fetch(leaf):
                re = h_spec[c, leaf // 2, re_at, leaf_lanes(leaf)].astype(F32)
                im = h_spec[c, leaf // 2, im_at, leaf_lanes(leaf)].astype(F32)
                cos, sin = twist[leaf, 0, re_at, :], twist[leaf, 1, re_at, :]
                return re * cos + im * sin, im * cos - re * sin

            parts = split_inverse(fetch, blocks, math.pi / 2, 0, True)
            for a, (re, _unused) in enumerate(parts):
                at = pl.ds(pl.multiple_of((a % tiles) * LANES + r * step, step), step)
                sig = recv[a // tiles, at, at_lanes].astype(F32)
                recv[a // tiles, at, at_lanes] = (re * (1.0 / length) + gain * sig).astype(BF16)
            return 0

        lax.fori_loop(0, LANES // step, back_step, 0)

        def return_step(d, _):
            out_copy(c, d).start()
            return 0

        lax.fori_loop(1, n, return_step, 0)
        own_out(c).start()

    for c in range(chunks):
        def q_step(i, _):
            peers = (2 * i, 2 * i + 1)
            taps = [short(0, slot, p, c) for slot, p in enumerate(peers)]
            for slot, p in enumerate(peers):
                parts = [sums_of(slot, taps[slot], start, part).astype(BF16) for start in range(0, tok, part)]
                out_ref[peer_rows(p, c), :] = across(eye[:lanes, :lanes], jnp.concatenate(parts, axis=0)).astype(BF16)
            return 0

        lax.fori_loop(0, n // 2, q_step, 0)

    def mix(peer, c):
        at = peer_rows(peer, c)
        long = across(eye[:lanes, :lanes], ret[peer, :, chunk_lanes(c)])
        out_ref[at, :] = (out_ref[at, :].astype(F32) * long).astype(BF16)

    for c in range(chunks):
        own_out(c).wait()
        mix(me, c)

        def mix_step(d, _):
            out_copy(c, d).wait()
            mix(lax.rem(me + n - d, n), c)
            return 0

        lax.fori_loop(1, n, mix_step, 0)


def solution(mesh):
    n = mesh.shape["ctx"]

    def local(queries, keys, values, short_taps, long_filter, skip_gain):
        width, tok = queries.shape
        chan, length = long_filter.shape[1:]
        blocks = length // LANES
        lanes = min(chan, LANES)
        chunks = chan // lanes
        table = jnp.asarray(circle_tables())
        columns = jnp.asarray(twist_columns(blocks))
        dma = pltpu.SemaphoreType.DMA
        two = 2 * LANES
        small = blocks * two * max(chan, LANES) * 4 <= 8 * 2**20
        side = max(tok, LANES)
        any_space = pl.BlockSpec(memory_space=pl.ANY)
        taps = short_taps
        if lanes < LANES:
            taps = jnp.moveaxis(short_taps.reshape(3, -1, n, chan), 2, 0)
        return pl.pallas_call(
            functools.partial(kernel, n, lanes),
            out_shape=jax.ShapeDtypeStruct((width, tok), BF16),
            in_specs=[any_space if i == 4 else pl.BlockSpec(memory_space=pltpu.VMEM) for i in range(8)],
            out_specs=pl.BlockSpec(memory_space=pltpu.VMEM),
            scratch_shapes=[
                pltpu.VMEM((side, side), BF16),
                pltpu.VMEM((3, n, SLOT, chan), BF16),
                pltpu.VMEM((3, n, SLOT, chan), BF16),
                pltpu.VMEM((4, SLOT + tok, lanes), F32),
                pltpu.VMEM((n, tok, chan), BF16),
                pltpu.VMEM((n, tok, chan), BF16),
                pltpu.VMEM((blocks // 2, two, two), BF16),
                pltpu.VMEM((chunks, blocks // 2, two, two), F32 if small else BF16),
                pltpu.VMEM((n, tok, chan), BF16),
                pltpu.VMEM((chan, length), BF16),
                pltpu.VMEM((n, tok, chan), BF16),
                pltpu.VMEM((blocks, 2, LANES, lanes), F32),
                dma,
                dma((2,)),
                dma((chunks, n)),
                dma((chunks, n)),
                dma((chunks,)),
                dma((chunks, n)),
                dma((chunks, n)),
                dma((chunks,)),
            ],
            compiler_params=pltpu.CompilerParams(
                collective_id=0, has_side_effects=True, vmem_limit_bytes=67043328
            ),
            name="hyena",
        )(queries, keys, values, taps, long_filter[0], skip_gain, table, columns)

    placed = (
        P("ch", "ctx"),
        P("ch", "ctx"),
        P("ch", "ctx"),
        P(None, None, "ch"),
        P("ch", "ctx", None),
        P("ch", "ctx"),
    )
    return jax.shard_map(local, mesh=mesh, in_specs=placed, out_specs=P("ch", "ctx"), check_vma=False)
```

```python
import functools
import math

import jax
import jax.numpy as jnp
import ml_dtypes
import numpy as np
from jax import lax
from jax.experimental import pallas as pl
from jax.experimental.pallas import tpu as pltpu
from jax.sharding import PartitionSpec as P

MESH = pl.DeviceIdType.MESH
LANES = 128
SLOT = 8
F32 = jnp.float32
BF16 = jnp.bfloat16


def leaf_angles(count, theta):
    if count == 1:
        return [theta]
    return leaf_angles(count // 2, theta / 2) + leaf_angles(count // 2, theta / 2 + math.pi)


def circle_tables():
    place = np.arange(LANES, dtype=np.float64)
    angle = place[:, None] * place[None, :] * (2.0 * math.pi / LANES)
    cos, sin = np.cos(angle), np.sin(angle)
    there = np.block([[cos, -sin], [sin, cos]])
    return np.stack([there, there.T]).astype(ml_dtypes.bfloat16)


def twist_columns(count):
    roots = np.array(leaf_angles(count, 0.0)) + math.pi / (2 * count)
    angle = np.arange(LANES)[:, None] * roots[None, :] / LANES
    return np.concatenate([np.cos(angle), np.sin(angle)], axis=1).astype(np.float32)


def turn(re, im, angle):
    eighth = round(angle / (math.pi / 4))
    if abs(angle - eighth * math.pi / 4) > 1e-9:
        cos, sin = math.cos(angle), math.sin(angle)
        return cos * re - sin * im, cos * im + sin * re
    eighth %= 8
    if eighth % 2:
        re, im = math.sqrt(0.5) * (re - im), math.sqrt(0.5) * (re + im)
    return [(re, im), (-im, re), (-re, -im), (im, -re)][eighth // 2]


def split_forward(coefs, theta, first, emit):
    count = len(coefs)
    if count == 1:
        emit(first, *coefs[0])
        return
    half = count // 2
    plus, minus = [], []
    for (lo_re, lo_im), high in zip(coefs[:half], coefs[half:]):
        hi_re, hi_im = turn(*high, theta / 2)
        plus.append((lo_re + hi_re, lo_im + hi_im))
        minus.append((lo_re - hi_re, lo_im - hi_im))
    split_forward(plus, theta / 2, first, emit)
    split_forward(minus, theta / 2 + math.pi, first + half, emit)


def split_inverse(fetch, count, theta, first):
    if count == 1:
        return [fetch(first)]
    half = count // 2
    plus = split_inverse(fetch, half, theta / 2, first)
    minus = split_inverse(fetch, half, theta / 2 + math.pi, first + half)
    low, high = [], []
    for (p_re, p_im), (m_re, m_im) in zip(plus, minus):
        low.append((p_re + m_re, p_im + m_im))
        high.append(turn(p_re - m_re, p_im - m_im, -theta / 2))
    return low + high


def across(eye, block):
    return lax.dot_general(eye, block, (((1,), (1,)), ((), ())), preferred_element_type=F32)


def kernel(
    n, lanes,
    q_ref, k_ref, v_ref, taps_ref, filt_hbm, gain_ref, table_ref, twist_ref,
    out_ref,
    eye, tails, halo, turned, gated, recv, spec, h_spec, ret, filt_ref, filt_rows, twist,
    filt_sem, halo_sem, in_send, in_recv, in_own, out_send, out_recv, out_own,
):
    me = lax.axis_index("ctx")
    width, tok = q_ref.shape
    chan, length = filt_ref.shape
    chunks = chan // lanes
    rim = taps_ref.shape[-2]
    blocks = length // LANES
    tiles = tok // LANES
    sources = (q_ref, k_ref, v_ref)
    step = 16
    filt_copy = pltpu.make_async_copy(filt_hbm, filt_ref, filt_sem)
    filt_copy.start()

    barrier = pltpu.get_barrier_semaphore()
    for d in range(1, n):
        pl.semaphore_signal(barrier, inc=1, device_id={"ctx": lax.rem(me + d, n)}, device_id_type=MESH)

    side = eye.shape[0]
    row = lax.broadcasted_iota(jnp.int32, (side, side), 0)
    col = lax.broadcasted_iota(jnp.int32, (side, side), 1)
    eye[...] = (row == col).astype(F32).astype(BF16)

    pick_row = lax.broadcasted_iota(jnp.int32, (SLOT, LANES), 0) + (LANES - SLOT)
    pick = (pick_row == lax.broadcasted_iota(jnp.int32, (SLOT, LANES), 1)).astype(F32).astype(BF16)

    def tail_step(p, _):
        at = pl.ds(pl.multiple_of(p * chan, chan), chan)
        for w in range(3):
            tails[w, p] = across(pick, sources[w][at, tok - LANES :]).astype(BF16)
        return 0

    lax.fori_loop(0, n, tail_step, 0, unroll=4)

    pl.semaphore_wait(barrier, n - 1)
    halo_copy = pltpu.make_async_remote_copy(
        src_ref=tails, dst_ref=halo, send_sem=halo_sem.at[0], recv_sem=halo_sem.at[1],
        device_id={"ctx": lax.rem(me + 1, n)}, device_id_type=MESH,
    )

    halo_copy.start()
    if lanes < LANES:
        spec[...] = jnp.zeros_like(spec)

    filt_copy.wait()
    for a in range(blocks):
        filt_rows[a // tiles, (a % tiles) * LANES : (a % tiles + 1) * LANES, :] = across(
            eye[:LANES, :LANES], filt_ref[:, a * LANES : (a + 1) * LANES]
        ).astype(BF16)

    def chunk_lanes(c):
        return slice(c * lanes, (c + 1) * lanes)

    def leaf_lanes(leaf):
        return slice((leaf % 2) * LANES, (leaf % 2) * LANES + lanes)

    def short_stage(ref, c, first=False):
        at_lanes = chunk_lanes(c)

        def one(r, _):
            re_at = pl.ds(pl.multiple_of(r * step, step), step)
            im_at = pl.ds(pl.multiple_of(LANES + r * step, step), step)

            def emit(leaf, re, im):
                if first:
                    for which in range(2):
                        column = twist_ref[re_at, which * blocks + leaf : which * blocks + leaf + 1]
                        twist[leaf, which, re_at, :] = jnp.broadcast_to(column, (step, lanes))
                cos, sin = twist[leaf, 0, re_at, :], twist[leaf, 1, re_at, :]
                spec[leaf // 2, re_at, leaf_lanes(leaf)] = (re * cos - im * sin).astype(BF16)
                spec[leaf // 2, im_at, leaf_lanes(leaf)] = (re * sin + im * cos).astype(BF16)

            coefs = []
            for a in range(blocks):
                at = pl.ds(pl.multiple_of((a % tiles) * LANES + r * step, step), step)
                x, lean = ref[a // tiles, at, at_lanes].astype(F32), a * math.pi / (2 * blocks)
                coefs.append((x * math.cos(lean), x * math.sin(lean)))
            split_forward(coefs, 0.0, 0, emit)
            return 0

        lax.fori_loop(0, LANES // step, one, 0)

    def filter_chunk(c):
        short_stage(filt_rows, c, c == 0)

        def filt_pair(pair, _):
            h_spec[c, pair] = jnp.dot(table_ref[0], spec[pair], preferred_element_type=F32).astype(h_spec.dtype)
            return 0

        lax.fori_loop(0, blocks // 2, filt_pair, 0, unroll=2)

    filter_chunk(0)
    halo_copy.wait()

    def peer_rows(peer, c):
        return pl.ds(pl.multiple_of(peer * chan + c * lanes, lanes), lanes)

    def short(first, pair, c):
        block = jnp.concatenate([sources[w][peer_rows(peer, c), :] for w, peer in pair], axis=0)
        both = across(eye[:tok, :tok], block)
        taps = []
        for i, (w, peer) in enumerate(pair):
            turned[first + i, :SLOT, :] = jnp.where(me > 0, halo[w, peer, :, chunk_lanes(c)].astype(F32), 0.0)
            turned[first + i, SLOT:, :] = both[:, i * lanes : (i + 1) * lanes]
            if len(taps_ref.shape) == 3:
                taps.append(taps_ref[w, :, peer_rows(peer, c)])
            else:
                taps.append(taps_ref[peer, w, :, chunk_lanes(c)])
        return taps

    def sums_of(slot, taps, start, count):
        total = None
        for j in range(rim):
            term = taps[j : j + 1, :] * turned[slot, SLOT - j + start : SLOT - j + start + count, :]
            total = term if total is None else total + term
        return total

    part = 64

    def gate_pair(peers, c):
        taps = [short(2 * i, [(1, p), (2, p)], c) for i, p in enumerate(peers)]
        for i, p in enumerate(peers):
            for start in range(0, tok, part):
                product = sums_of(2 * i, taps[i][0], start, part) * sums_of(2 * i + 1, taps[i][1], start, part)
                gated[p, start : start + part, chunk_lanes(c)] = product.astype(BF16)

    def in_copy(c, d):
        peer = lax.rem(me + d, n)
        return pltpu.make_async_remote_copy(
            src_ref=gated.at[peer, :, chunk_lanes(c)], dst_ref=recv.at[me, :, chunk_lanes(c)],
            send_sem=in_send.at[c, d], recv_sem=in_recv.at[c, d],
            device_id={"ctx": peer}, device_id_type=MESH,
        )

    def own_in(c):
        return pltpu.make_async_copy(gated.at[me, :, chunk_lanes(c)], recv.at[me, :, chunk_lanes(c)], in_own.at[c])

    def out_copy(c, d):
        peer = lax.rem(me + d, n)
        return pltpu.make_async_remote_copy(
            src_ref=recv.at[peer, :, chunk_lanes(c)], dst_ref=ret.at[me, :, chunk_lanes(c)],
            send_sem=out_send.at[c, d], recv_sem=out_recv.at[c, d],
            device_id={"ctx": peer}, device_id_type=MESH,
        )

    def own_out(c):
        return pltpu.make_async_copy(recv.at[me, :, chunk_lanes(c)], ret.at[me, :, chunk_lanes(c)], out_own.at[c])

    for c in range(chunks):
        def send_step(i, _):
            gate_pair([lax.rem(me + 2 * i + 1, n), lax.rem(me + 2 * i + 2, n)], c)

            @pl.when(i > 0)
            def _():
                in_copy(c, 2 * i - 1).start()
                in_copy(c, 2 * i).start()

            return 0

        lax.fori_loop(0, n // 2, send_step, 0)
        in_copy(c, n - 1).start()
        own_in(c).start()

    for c in range(1, chunks):
        filter_chunk(c)

    for c in range(chunks):
        def wait_in(d, _):
            in_copy(c, d).wait()
            return 0

        lax.fori_loop(1, n, wait_in, 0)
        own_in(c).wait()
        at_lanes = chunk_lanes(c)
        short_stage(recv, c)

        def pair_step(pair, _):
            sig = jnp.dot(table_ref[0], spec[pair], preferred_element_type=F32)
            h_re, h_im = h_spec[c, pair, :LANES, :].astype(F32), h_spec[c, pair, LANES:, :].astype(F32)
            s_re, s_im = sig[:LANES], sig[LANES:]
            prod = jnp.concatenate([s_re * h_re - s_im * h_im, s_re * h_im + s_im * h_re], axis=0).astype(BF16)
            h_spec[c, pair] = jnp.dot(table_ref[1], prod, preferred_element_type=F32).astype(h_spec.dtype)
            return 0

        lax.fori_loop(0, blocks // 2, pair_step, 0, unroll=4)
        gain = gain_ref[:, at_lanes]

        def back_step(r, _):
            re_at = pl.ds(pl.multiple_of(r * step, step), step)
            im_at = pl.ds(pl.multiple_of(LANES + r * step, step), step)
            def fetch(leaf):
                re = h_spec[c, leaf // 2, re_at, leaf_lanes(leaf)].astype(F32)
                im = h_spec[c, leaf // 2, im_at, leaf_lanes(leaf)].astype(F32)
                cos, sin = twist[leaf, 0, re_at, :], twist[leaf, 1, re_at, :]
                return re * cos + im * sin, im * cos - re * sin

            parts = split_inverse(fetch, blocks, 0.0, 0)
            for a, (re, im) in enumerate(parts):
                lean = a * math.pi / (2 * blocks)
                cos, sin = math.cos(lean) / length, math.sin(lean) / length
                at = pl.ds(pl.multiple_of((a % tiles) * LANES + r * step, step), step)
                sig = recv[a // tiles, at, at_lanes].astype(F32)
                recv[a // tiles, at, at_lanes] = (cos * re + sin * im + gain * sig).astype(BF16)
            return 0

        lax.fori_loop(0, LANES // step, back_step, 0)

        def return_step(d, _):
            out_copy(c, d).start()
            return 0

        lax.fori_loop(1, n, return_step, 0)
        own_out(c).start()

    for c in range(chunks):
        def q_step(i, _):
            peers = (2 * i, 2 * i + 1)
            taps = short(0, [(0, p) for p in peers], c)
            for slot, p in enumerate(peers):
                parts = [sums_of(slot, taps[slot], start, part).astype(BF16) for start in range(0, tok, part)]
                out_ref[peer_rows(p, c), :] = across(eye[:lanes, :lanes], jnp.concatenate(parts, axis=0)).astype(BF16)
            return 0

        lax.fori_loop(0, n // 2, q_step, 0)

    def mix(peer, c):
        at = peer_rows(peer, c)
        long = across(eye[:lanes, :lanes], ret[peer, :, chunk_lanes(c)])
        out_ref[at, :] = (out_ref[at, :].astype(F32) * long).astype(BF16)

    for c in range(chunks):
        own_out(c).wait()
        mix(me, c)

        def mix_step(d, _):
            out_copy(c, d).wait()
            mix(lax.rem(me + n - d, n), c)
            return 0

        lax.fori_loop(1, n, mix_step, 0)


def solution(mesh):
    n = mesh.shape["ctx"]

    def local(queries, keys, values, short_taps, long_filter, skip_gain):
        width, tok = queries.shape
        chan, length = long_filter.shape[1:]
        blocks = length // LANES
        lanes = min(chan, LANES)
        chunks = chan // lanes
        table = jnp.asarray(circle_tables())
        twist = jnp.asarray(twist_columns(blocks))
        dma = pltpu.SemaphoreType.DMA
        two = 2 * LANES
        small = blocks * two * max(chan, LANES) * 4 <= 8 * 2**20
        side = max(tok, LANES)
        any_space = pl.BlockSpec(memory_space=pl.ANY)
        taps = short_taps
        if lanes < LANES:
            taps = jnp.moveaxis(short_taps.reshape(3, -1, n, chan), 2, 0)
        return pl.pallas_call(
            functools.partial(kernel, n, lanes),
            out_shape=jax.ShapeDtypeStruct((width, tok), BF16),
            in_specs=[any_space if i == 4 else pl.BlockSpec(memory_space=pltpu.VMEM) for i in range(8)],
            out_specs=pl.BlockSpec(memory_space=pltpu.VMEM),
            scratch_shapes=[
                pltpu.VMEM((side, side), BF16),
                pltpu.VMEM((3, n, SLOT, chan), BF16),
                pltpu.VMEM((3, n, SLOT, chan), BF16),
                pltpu.VMEM((4, SLOT + tok, lanes), F32),
                pltpu.VMEM((n, tok, chan), BF16),
                pltpu.VMEM((n, tok, chan), BF16),
                pltpu.VMEM((blocks // 2, two, two), BF16),
                pltpu.VMEM((chunks, blocks // 2, two, two), F32 if small else BF16),
                pltpu.VMEM((n, tok, chan), BF16),
                pltpu.VMEM((chan, length), BF16),
                pltpu.VMEM((n, tok, chan), BF16),
                pltpu.VMEM((blocks, 2, LANES, lanes), F32),
                dma,
                dma((2,)),
                dma((chunks, n)),
                dma((chunks, n)),
                dma((chunks,)),
                dma((chunks, n)),
                dma((chunks, n)),
                dma((chunks,)),
            ],
            compiler_params=pltpu.CompilerParams(
                collective_id=0, has_side_effects=True, vmem_limit_bytes=67043328
            ),
            name="hyena",
        )(queries, keys, values, taps, long_filter[0], skip_gain, table, twist)

    placed = (
        P("ch", "ctx"),
        P("ch", "ctx"),
        P("ch", "ctx"),
        P(None, None, "ch"),
        P("ch", "ctx", None),
        P("ch", "ctx"),
    )
    return jax.shard_map(local, mesh=mesh, in_specs=placed, out_specs=P("ch", "ctx"), check_vma=False)
```

```python
import functools
import math

import jax
import jax.numpy as jnp
import ml_dtypes
import numpy as np
from jax import lax
from jax.experimental import pallas as pl
from jax.experimental.pallas import tpu as pltpu
from jax.sharding import PartitionSpec as P

MESH = pl.DeviceIdType.MESH
LANES = 128
SLOT = 8
F32 = jnp.float32
BF16 = jnp.bfloat16


def leaf_angles(count, theta):
    if count == 1:
        return [theta]
    return leaf_angles(count // 2, theta / 2) + leaf_angles(count // 2, theta / 2 + math.pi)


def circle_tables():
    place = np.arange(LANES, dtype=np.float64)
    angle = place[:, None] * place[None, :] * (2.0 * math.pi / LANES)
    cos, sin = np.cos(angle), np.sin(angle)
    there = np.block([[cos, -sin], [sin, cos]])
    return np.stack([there, there.T]).astype(ml_dtypes.bfloat16)


def twist_columns(count):
    roots = np.array(leaf_angles(count, 0.0)) + math.pi / (2 * count)
    angle = np.arange(LANES)[:, None] * roots[None, :] / LANES
    return np.concatenate([np.cos(angle), np.sin(angle)], axis=1).astype(np.float32)


def turn(re, im, angle):
    eighth = round(angle / (math.pi / 4))
    if abs(angle - eighth * math.pi / 4) > 1e-9:
        cos, sin = math.cos(angle), math.sin(angle)
        return cos * re - sin * im, cos * im + sin * re
    eighth %= 8
    if eighth % 2:
        re, im = math.sqrt(0.5) * (re - im), math.sqrt(0.5) * (re + im)
    return [(re, im), (-im, re), (-re, -im), (im, -re)][eighth // 2]


def split_forward(coefs, theta, first, emit):
    count = len(coefs)
    if count == 1:
        emit(first, *coefs[0])
        return
    half = count // 2
    plus, minus = [], []
    for (lo_re, lo_im), high in zip(coefs[:half], coefs[half:]):
        hi_re, hi_im = turn(*high, theta / 2)
        plus.append((lo_re + hi_re, lo_im + hi_im))
        minus.append((lo_re - hi_re, lo_im - hi_im))
    split_forward(plus, theta / 2, first, emit)
    split_forward(minus, theta / 2 + math.pi, first + half, emit)


def split_inverse(fetch, count, theta, first):
    if count == 1:
        return [fetch(first)]
    half = count // 2
    plus = split_inverse(fetch, half, theta / 2, first)
    minus = split_inverse(fetch, half, theta / 2 + math.pi, first + half)
    low, high = [], []
    for (p_re, p_im), (m_re, m_im) in zip(plus, minus):
        low.append((p_re + m_re, p_im + m_im))
        high.append(turn(p_re - m_re, p_im - m_im, -theta / 2))
    return low + high


def across(eye, block):
    return lax.dot_general(eye, block, (((1,), (1,)), ((), ())), preferred_element_type=F32)


def kernel(
    n, lanes,
    q_ref, k_ref, v_ref, taps_ref, filt_hbm, gain_ref, table_ref, twist_ref,
    out_hbm,
    out_ref, eye, tails, halo, turned, gated, recv, spec, h_spec, ret, filt_ref, filt_rows, twist,
    filt_sem, halo_sem, in_send, in_recv, in_own, out_send, out_recv, out_own, put,
):
    me = lax.axis_index("ctx")
    width, tok = q_ref.shape
    chan, length = filt_ref.shape
    chunks = chan // lanes
    rim = taps_ref.shape[-2]
    blocks = length // LANES
    tiles = tok // LANES
    sources = (q_ref, k_ref, v_ref)
    step = 16
    filt_copy = pltpu.make_async_copy(filt_hbm, filt_ref, filt_sem)
    filt_copy.start()

    barrier = pltpu.get_barrier_semaphore()
    for d in range(1, n):
        pl.semaphore_signal(barrier, inc=1, device_id={"ctx": lax.rem(me + d, n)}, device_id_type=MESH)

    side = eye.shape[0]
    row = lax.broadcasted_iota(jnp.int32, (side, side), 0)
    col = lax.broadcasted_iota(jnp.int32, (side, side), 1)
    eye[...] = (row == col).astype(F32).astype(BF16)

    pick_row = lax.broadcasted_iota(jnp.int32, (SLOT, LANES), 0) + (LANES - SLOT)
    pick = (pick_row == lax.broadcasted_iota(jnp.int32, (SLOT, LANES), 1)).astype(F32).astype(BF16)

    def tail_step(p, _):
        at = pl.ds(pl.multiple_of(p * chan, chan), chan)
        for w in range(3):
            tails[w, p] = across(pick, sources[w][at, tok - LANES :]).astype(BF16)
        return 0

    lax.fori_loop(0, n, tail_step, 0, unroll=4)

    pl.semaphore_wait(barrier, n - 1)
    halo_copy = pltpu.make_async_remote_copy(
        src_ref=tails, dst_ref=halo, send_sem=halo_sem.at[0], recv_sem=halo_sem.at[1],
        device_id={"ctx": lax.rem(me + 1, n)}, device_id_type=MESH,
    )

    halo_copy.start()
    if lanes < LANES:
        spec[...] = jnp.zeros_like(spec)

    filt_copy.wait()
    for a in range(blocks):
        filt_rows[a // tiles, (a % tiles) * LANES : (a % tiles + 1) * LANES, :] = across(
            eye[:LANES, :LANES], filt_ref[:, a * LANES : (a + 1) * LANES]
        ).astype(BF16)

    def chunk_lanes(c):
        return slice(c * lanes, (c + 1) * lanes)

    def leaf_lanes(leaf):
        return slice((leaf % 2) * LANES, (leaf % 2) * LANES + lanes)

    def short_stage(ref, c, first=False):
        at_lanes = chunk_lanes(c)

        def one(r, _):
            re_at = pl.ds(pl.multiple_of(r * step, step), step)
            im_at = pl.ds(pl.multiple_of(LANES + r * step, step), step)

            def emit(leaf, re, im):
                if first:
                    for which in range(2):
                        column = twist_ref[re_at, which * blocks + leaf : which * blocks + leaf + 1]
                        twist[leaf, which, re_at, :] = jnp.broadcast_to(column, (step, lanes))
                cos, sin = twist[leaf, 0, re_at, :], twist[leaf, 1, re_at, :]
                spec[leaf // 2, re_at, leaf_lanes(leaf)] = (re * cos - im * sin).astype(BF16)
                spec[leaf // 2, im_at, leaf_lanes(leaf)] = (re * sin + im * cos).astype(BF16)

            coefs = []
            for a in range(blocks):
                at = pl.ds(pl.multiple_of((a % tiles) * LANES + r * step, step), step)
                x, lean = ref[a // tiles, at, at_lanes].astype(F32), a * math.pi / (2 * blocks)
                coefs.append((x * math.cos(lean), x * math.sin(lean)))
            split_forward(coefs, 0.0, 0, emit)
            return 0

        lax.fori_loop(0, LANES // step, one, 0)

    def filter_chunk(c):
        short_stage(filt_rows, c, c == 0)

        def filt_pair(pair, _):
            h_spec[c, pair] = jnp.dot(table_ref[0], spec[pair], preferred_element_type=F32).astype(h_spec.dtype)
            return 0

        lax.fori_loop(0, blocks // 2, filt_pair, 0, unroll=2)

    filter_chunk(0)
    halo_copy.wait()

    def peer_rows(peer, c):
        return pl.ds(pl.multiple_of(peer * chan + c * lanes, lanes), lanes)

    def short(first, pair, c):
        block = jnp.concatenate([sources[w][peer_rows(peer, c), :] for w, peer in pair], axis=0)
        both = across(eye[:tok, :tok], block)
        taps = []
        for i, (w, peer) in enumerate(pair):
            turned[first + i, :SLOT, :] = jnp.where(me > 0, halo[w, peer, :, chunk_lanes(c)].astype(F32), 0.0)
            turned[first + i, SLOT:, :] = both[:, i * lanes : (i + 1) * lanes]
            if len(taps_ref.shape) == 3:
                taps.append(taps_ref[w, :, peer_rows(peer, c)])
            else:
                taps.append(taps_ref[peer, w, :, chunk_lanes(c)])
        return taps

    def sums_of(slot, taps, start, count):
        total = None
        for j in range(rim):
            term = taps[j : j + 1, :] * turned[slot, SLOT - j + start : SLOT - j + start + count, :]
            total = term if total is None else total + term
        return total

    part = 64

    def gate_pair(peers, c):
        taps = [short(2 * i, [(1, p), (2, p)], c) for i, p in enumerate(peers)]
        for i, p in enumerate(peers):
            for start in range(0, tok, part):
                product = sums_of(2 * i, taps[i][0], start, part) * sums_of(2 * i + 1, taps[i][1], start, part)
                gated[p, start : start + part, chunk_lanes(c)] = product.astype(BF16)

    def in_copy(c, d):
        peer = lax.rem(me + d, n)
        return pltpu.make_async_remote_copy(
            src_ref=gated.at[peer, :, chunk_lanes(c)], dst_ref=recv.at[me, :, chunk_lanes(c)],
            send_sem=in_send.at[c, d], recv_sem=in_recv.at[c, d],
            device_id={"ctx": peer}, device_id_type=MESH,
        )

    def own_in(c):
        return pltpu.make_async_copy(gated.at[me, :, chunk_lanes(c)], recv.at[me, :, chunk_lanes(c)], in_own.at[c])

    def out_copy(c, d):
        peer = lax.rem(me + d, n)
        return pltpu.make_async_remote_copy(
            src_ref=recv.at[peer, :, chunk_lanes(c)], dst_ref=ret.at[me, :, chunk_lanes(c)],
            send_sem=out_send.at[c, d], recv_sem=out_recv.at[c, d],
            device_id={"ctx": peer}, device_id_type=MESH,
        )

    def own_out(c):
        return pltpu.make_async_copy(recv.at[me, :, chunk_lanes(c)], ret.at[me, :, chunk_lanes(c)], out_own.at[c])

    for c in range(chunks):
        def send_step(i, _):
            gate_pair([lax.rem(me + 2 * i + 1, n), lax.rem(me + 2 * i + 2, n)], c)

            @pl.when(i > 0)
            def _():
                in_copy(c, 2 * i - 1).start()
                in_copy(c, 2 * i).start()

            return 0

        lax.fori_loop(0, n // 2, send_step, 0)
        in_copy(c, n - 1).start()
        own_in(c).start()

    for c in range(1, chunks):
        filter_chunk(c)

    for c in range(chunks):
        def wait_in(d, _):
            in_copy(c, d).wait()
            return 0

        lax.fori_loop(1, n, wait_in, 0)
        own_in(c).wait()
        at_lanes = chunk_lanes(c)
        short_stage(recv, c)

        def pair_step(pair, _):
            sig = jnp.dot(table_ref[0], spec[pair], preferred_element_type=F32)
            h_re, h_im = h_spec[c, pair, :LANES, :].astype(F32), h_spec[c, pair, LANES:, :].astype(F32)
            s_re, s_im = sig[:LANES], sig[LANES:]
            prod = jnp.concatenate([s_re * h_re - s_im * h_im, s_re * h_im + s_im * h_re], axis=0).astype(BF16)
            h_spec[c, pair] = jnp.dot(table_ref[1], prod, preferred_element_type=F32).astype(h_spec.dtype)
            return 0

        lax.fori_loop(0, blocks // 2, pair_step, 0, unroll=4)
        gain = gain_ref[:, at_lanes]

        def back_step(r, _):
            re_at = pl.ds(pl.multiple_of(r * step, step), step)
            im_at = pl.ds(pl.multiple_of(LANES + r * step, step), step)
            def fetch(leaf):
                re = h_spec[c, leaf // 2, re_at, leaf_lanes(leaf)].astype(F32)
                im = h_spec[c, leaf // 2, im_at, leaf_lanes(leaf)].astype(F32)
                cos, sin = twist[leaf, 0, re_at, :], twist[leaf, 1, re_at, :]
                return re * cos + im * sin, im * cos - re * sin

            parts = split_inverse(fetch, blocks, 0.0, 0)
            for a, (re, im) in enumerate(parts):
                lean = a * math.pi / (2 * blocks)
                cos, sin = math.cos(lean) / length, math.sin(lean) / length
                at = pl.ds(pl.multiple_of((a % tiles) * LANES + r * step, step), step)
                sig = recv[a // tiles, at, at_lanes].astype(F32)
                recv[a // tiles, at, at_lanes] = (cos * re + sin * im + gain * sig).astype(BF16)
            return 0

        lax.fori_loop(0, LANES // step, back_step, 0)

        def return_step(d, _):
            out_copy(c, d).start()
            return 0

        lax.fori_loop(1, n, return_step, 0)
        own_out(c).start()

    for c in range(chunks):
        def q_step(i, _):
            peers = (2 * i, 2 * i + 1)
            taps = short(0, [(0, p) for p in peers], c)
            for slot, p in enumerate(peers):
                parts = [sums_of(slot, taps[slot], start, part).astype(BF16) for start in range(0, tok, part)]
                out_ref[peer_rows(p, c), :] = across(eye[:lanes, :lanes], jnp.concatenate(parts, axis=0)).astype(BF16)
            return 0

        lax.fori_loop(0, n // 2, q_step, 0)

    def mix(peer, c):
        at = peer_rows(peer, c)
        long = across(eye[:lanes, :lanes], ret[peer, :, chunk_lanes(c)])
        out_ref[at, :] = (out_ref[at, :].astype(F32) * long).astype(BF16)
        put_copy(peer, c).start()

    def put_copy(peer, c):
        at = peer_rows(peer, c)
        return pltpu.make_async_copy(out_ref.at[at, :], out_hbm.at[at, :], put.at[c, peer])

    for c in range(chunks):
        own_out(c).wait()
        mix(me, c)

        def mix_step(d, _):
            out_copy(c, d).wait()
            mix(lax.rem(me + n - d, n), c)
            return 0

        lax.fori_loop(1, n, mix_step, 0)

    for c in range(chunks):
        def put_step(p, _):
            put_copy(p, c).wait()
            return 0

        lax.fori_loop(0, n, put_step, 0)


def solution(mesh):
    n = mesh.shape["ctx"]

    def local(queries, keys, values, short_taps, long_filter, skip_gain):
        width, tok = queries.shape
        chan, length = long_filter.shape[1:]
        blocks = length // LANES
        lanes = min(chan, LANES)
        chunks = chan // lanes
        table = jnp.asarray(circle_tables())
        twist = jnp.asarray(twist_columns(blocks))
        dma = pltpu.SemaphoreType.DMA
        two = 2 * LANES
        small = blocks * two * max(chan, LANES) * 4 <= 8 * 2**20
        side = max(tok, LANES)
        any_space = pl.BlockSpec(memory_space=pl.ANY)
        taps = short_taps
        if lanes < LANES:
            taps = jnp.moveaxis(short_taps.reshape(3, -1, n, chan), 2, 0)
        return pl.pallas_call(
            functools.partial(kernel, n, lanes),
            out_shape=jax.ShapeDtypeStruct((width, tok), BF16),
            in_specs=[any_space if i == 4 else pl.BlockSpec(memory_space=pltpu.VMEM) for i in range(8)],
            out_specs=any_space,
            scratch_shapes=[
                pltpu.VMEM((width, tok), BF16),
                pltpu.VMEM((side, side), BF16),
                pltpu.VMEM((3, n, SLOT, chan), BF16),
                pltpu.VMEM((3, n, SLOT, chan), BF16),
                pltpu.VMEM((4, SLOT + tok, lanes), F32),
                pltpu.VMEM((n, tok, chan), BF16),
                pltpu.VMEM((n, tok, chan), BF16),
                pltpu.VMEM((blocks // 2, two, two), BF16),
                pltpu.VMEM((chunks, blocks // 2, two, two), F32 if small else BF16),
                pltpu.VMEM((n, tok, chan), BF16),
                pltpu.VMEM((chan, length), BF16),
                pltpu.VMEM((n, tok, chan), BF16),
                pltpu.VMEM((blocks, 2, LANES, lanes), F32),
                dma,
                dma((2,)),
                dma((chunks, n)),
                dma((chunks, n)),
                dma((chunks,)),
                dma((chunks, n)),
                dma((chunks, n)),
                dma((chunks,)),
                dma((chunks, n)),
            ],
            compiler_params=pltpu.CompilerParams(
                collective_id=0, has_side_effects=True, vmem_limit_bytes=67043328
            ),
            name="hyena",
        )(queries, keys, values, taps, long_filter[0], skip_gain, table, twist)

    placed = (
        P("ch", "ctx"),
        P("ch", "ctx"),
        P("ch", "ctx"),
        P(None, None, "ch"),
        P("ch", "ctx", None),
        P("ch", "ctx"),
    )
    return jax.shard_map(local, mesh=mesh, in_specs=placed, out_specs=P("ch", "ctx"), check_vma=False)
```
